32 devices in a mesh: fsdp: 4 (over y, x), ctx: 4 (over z), tp: 2 (over core).
Axes of the slice: x: 2, y: 2, z: 4, core: 2. Of those that a mesh axis runs over, the one named last changes fastest.
Arguments:
- tokens: bfloat16 [3, 4, 2048, 1536], P(None, 'fsdp', 'ctx'), may hold values from -6 to 6
- doc_lengths: int32 [3, 4, 2], P(None, 'fsdp'), may hold values from 1 to 1536, 2048 in all within a row
- token_order: int32 [3, 4, 2048], P(None, 'fsdp'), may hold values from 0 to 2047, each once within a row
- mixer_gain: bfloat16 [1536], P('fsdp'), may hold values from 0.5 to 1.5
- in_weight: bfloat16 [1536, 3, 1536], P('fsdp', None, 'tp'), may hold values from -0.15625 to 0.15625
- conv_kernel: bfloat16 [1536, 3], P('tp'), may hold values from -3.5 to 3.5
- out_weight: bfloat16 [1536, 1536], P('fsdp', 'tp'), may hold values from -0.15625 to 0.15625
- feed_gain: bfloat16 [1536], P('fsdp'), may hold values from 0.5 to 1.5
- gate_weight: bfloat16 [1536, 6912], P('fsdp', 'tp'), may hold values from -0.15625 to 0.15625
- up_weight: bfloat16 [1536, 6912], P('fsdp', 'tp'), may hold values from -0.15625 to 0.15625
- down_weight: bfloat16 [1536, 6912], P('fsdp', 'tp'), may hold values from -0.078125 to 0.078125
- cotangent: bfloat16 [3, 4, 2048, 1536], P(None, 'fsdp', 'ctx'), may hold values from -6 to 6
Outputs:
- block_out: bfloat16 [3, 4, 2048, 1536], P(None, 'fsdp', 'ctx')
- input_grad: bfloat16 [3, 4, 2048, 1536], P(None, 'fsdp', 'ctx')
- in_weight_grad: float32 [1536, 3, 1536], P(('fsdp', 'ctx'), None, 'tp')
- kernel_grad: float32 [2, 768, 3], P('tp', ('fsdp', 'ctx'))
- out_weight_grad: float32 [1536, 1536], P(('fsdp', 'ctx'), 'tp')
- gate_weight_grad: float32 [1536, 6912], P(('fsdp', 'ctx'), 'tp')
- up_weight_grad: float32 [1536, 6912], P(('fsdp', 'ctx'), 'tp')
- down_weight_grad: float32 [1536, 6912], P(('fsdp', 'ctx'), 'tp')
- mixer_gain_grad: float32 [1536], P(('fsdp', 'ctx'))
- feed_gain_grad: float32 [1536], P(('fsdp', 'ctx'))
The draws below stay inside these ranges and needn't reach their ends.
Inputs may be any that keep to these rules, and one draw needn't show every extreme that they name: `doc_lengths`: each row of 2 lengths sums to 2048, and its largest entry is at most 1536. `token_order`: each row is a permutation of the 2048 positions of a stream.
All inputs are finite; a program needn't handle non-finite values.
Results may differ from the reference program's by a relative error of at most 0.013.
Values may be sent and summed in bfloat16 or wider, within the bound.
No kernel may reach another device: no remote copies, remote signals or barrier semaphores. Data moves between devices by JAX's collectives and lax.ppermute only.
A program may use at most 384 MiB of HBM per device.

```python
import math
import jax
import jax.numpy as jnp
import numpy as np
from jax import lax

D = 1536
FF = 6912
KERNEL = 3
MB = 3
NDOC = 2
CTX_TOK = 2048
LONGEST = 1536
STREAMS = 4
N_TP = 2


def block_scale(stream_key, shape, shards, low, high):
    level, own = 1.0, jax.random.fold_in(stream_key, 6)
    for position, parts in shards:
        draws = jnp.exp(jax.random.uniform(jax.random.fold_in(own, position), (parts,), jnp.float32, low / len(shards), high / len(shards)))
        level = level * jnp.repeat(draws, shape[position] // parts).reshape([-1 if axis == position else 1 for axis in range(len(shape))])
    return level


def length_profile(amount, total, most, lean):
    loads = [(1 << 20) // math.isqrt(rank ** lean) + 1 for rank in range(2, amount + 1)]
    rest, given = total - most - (amount - 1), [1] * (amount - 1)
    while rest > 0:
        candidates = [i for i in range(amount - 1) if given[i] < most]
        pool, left = sum([loads[i] for i in candidates]), rest
        for i in candidates:
            extra = min(most - given[i], max(1, left * loads[i] // pool), rest)
            given[i] = given[i] + extra
            rest = rest - extra
    return np.array([most] + given)


def uneven_parts(rng, count, total, limit, skew):
    if count == 2:
        one = jax.random.randint(rng, (), max(1, total - limit), min(limit, total - 1) + 1)
        return jnp.stack([one, total - one])
    tallies = jnp.asarray(length_profile(count, total, limit, skew), jnp.int32)
    pairs = (count - 1) // 2
    source_of, taker = tallies[1:1 + 2 * pairs:2], tallies[2:2 + 2 * pairs:2]
    slack = jnp.minimum(source_of - 1, limit - taker)
    passed = jax.random.randint(jax.random.fold_in(rng, 1), (pairs,), 0, 1 << 20) % (slack + 1)
    tallies = tallies.at[1:1 + 2 * pairs:2].set(source_of - passed).at[2:2 + 2 * pairs:2].set(taker + passed)
    return tallies[jax.random.permutation(jax.random.fold_in(rng, 2), count)]


def scatter_about(rng, dims, deviation, reach, pieces=(), kind=jnp.bfloat16):
    values = jax.random.normal(rng, dims, jnp.float32) * deviation
    if len(pieces) > 0:
        values = block_scale(rng, dims, pieces, -0.22, 0.18) * values
    return jnp.clip(values, min=-reach, max=reach).astype(kind)


def setup_inputs(seed: int = 0) -> dict:
    key_list = jax.random.split(jax.random.key(seed), 13)
    tokens = scatter_about(key_list[0], (MB, STREAMS, CTX_TOK, D), 1.0, 6.0, ((1, 4), (2, 4)))
    doc_lengths = jax.vmap(lambda own: uneven_parts(own, NDOC, CTX_TOK, LONGEST, 2))(jax.random.split(key_list[1], MB * STREAMS)).reshape((MB, STREAMS, NDOC)).astype(jnp.int32)
    token_order = jax.vmap(lambda own: jax.random.permutation(own, CTX_TOK))(jax.random.split(key_list[2], MB * STREAMS)).reshape((MB, STREAMS, CTX_TOK)).astype(jnp.int32)
    mixer_gain = jnp.clip(1.0 + 0.1 * jax.random.normal(key_list[3], (D,), jnp.float32), 0.5, 1.5).astype(jnp.bfloat16)
    in_weight = scatter_about(key_list[4], (D, 3, D), D ** -0.5, 0.15625, ((0, 4), (2, 2)))
    conv_kernel = scatter_about(key_list[5], (D, KERNEL), KERNEL ** -0.5, 3.5, ((0, 2),))
    out_weight = scatter_about(key_list[6], (D, D), D ** -0.5, 0.15625, ((0, 4), (1, 2)))
    feed_gain = jnp.clip(1.0 + 0.1 * jax.random.normal(key_list[7], (D,), jnp.float32), 0.5, 1.5).astype(jnp.bfloat16)
    gate_weight = scatter_about(key_list[8], (D, FF), D ** -0.5, 0.15625, ((0, 4), (1, 2)))
    up_weight = scatter_about(key_list[9], (D, FF), D ** -0.5, 0.15625, ((0, 4), (1, 2)))
    down_weight = scatter_about(key_list[10], (D, FF), FF ** -0.5, 0.078125, ((0, 4), (1, 2)))
    cotangent = scatter_about(key_list[11], (MB, STREAMS, CTX_TOK, D), 1.0, 6.0, ((1, 4), (2, 4)))
    return dict(tokens=tokens, doc_lengths=doc_lengths, token_order=token_order, mixer_gain=mixer_gain, in_weight=in_weight, conv_kernel=conv_kernel, out_weight=out_weight, feed_gain=feed_gain, gate_weight=gate_weight, up_weight=up_weight, down_weight=down_weight, cotangent=cotangent)


norm_eps = 1e-05
highest = lax.Precision.HIGHEST

@jax.custom_vjp
def low(v):
    return lax.optimization_barrier(v.astype(jnp.bfloat16)).astype(jnp.float32)

@jax.custom_vjp
def low_back(v):
    return v

def low_keep(v):
    return (low(v), None)

def low_pass(kept, grad):
    return (grad,)

def back_keep(v):
    return (v, None)

def back_low(kept, grad):
    return (low(grad),)
low.defvjp(low_keep, low_pass)
low_back.defvjp(back_keep, back_low)

def start_flags(positions, offsets):
    return jnp.any(positions[..., :, None] == offsets[..., None, :], axis=-1).astype(jnp.float32)

def keep_masks(positions, offsets):
    running = jnp.ones(positions.shape, jnp.float32)
    keep_list = [running]
    for lag_step in range(1, KERNEL):
        running = running * (1.0 - start_flags(positions - (lag_step - 1), offsets))
        keep_list.append(running)
    return keep_list

def shifted(values, lag_step):
    padding = jnp.zeros((lag_step,) + values.shape[1:], values.dtype)
    return jnp.concatenate([padding, values[:values.shape[0] - lag_step]], axis=0)

def stream_pass(weights_all, packed, keep_list):
    in_weight, conv_kernel, out_weight, gate_weight, up_weight, down_weight, mixer_gain, feed_gain = weights_all
    scale_one = lax.rsqrt(lax.optimization_barrier(jnp.mean(packed * packed, axis=1, keepdims=True)) + norm_eps)
    normed_one = low(packed * scale_one * mixer_gain)
    streams = low_back(jnp.einsum('pd,dsc->psc', normed_one, in_weight, precision=highest))
    b_part = streams[:, 0]
    c_part = streams[:, 1]
    x_part = streams[:, 2]
    mixed_in = b_part * x_part
    conv_out = mixed_in * conv_kernel[:, 0]
    for lag_step in range(1, KERNEL):
        conv_out = conv_out + keep_list[lag_step][:, None] * shifted(mixed_in, lag_step) * conv_kernel[:, lag_step]
    gated = low(c_part * conv_out)
    resid = packed + low_back(jnp.dot(gated, out_weight.T, precision=highest))
    scale_two = lax.rsqrt(lax.optimization_barrier(jnp.mean(resid * resid, axis=1, keepdims=True)) + norm_eps)
    normed_two = low(resid * scale_two * feed_gain)
    gate_proj = low_back(jnp.dot(normed_two, gate_weight, precision=highest))
    up_proj = low_back(jnp.dot(normed_two, up_weight, precision=highest))
    hidden = low(jax.nn.silu(gate_proj) * up_proj)
    return resid + low_back(jnp.dot(hidden, down_weight.T, precision=highest))

def reference(tokens, doc_lengths, token_order, mixer_gain, in_weight, conv_kernel, out_weight, feed_gain, gate_weight, up_weight, down_weight, cotangent):
    weights_all = tuple((w.astype(jnp.float32) for w in (in_weight, conv_kernel, out_weight, gate_weight, up_weight, down_weight, mixer_gain, feed_gain)))
    stream_count = MB * STREAMS
    flat_tokens = tokens.reshape(stream_count, CTX_TOK, D)
    flat_cot = cotangent.reshape(stream_count, CTX_TOK, D)
    flat_order = token_order.reshape(stream_count, CTX_TOK)
    flat_lengths = doc_lengths.reshape(stream_count, NDOC)
    positions = jnp.arange(CTX_TOK, dtype=jnp.int32)

    def one_stream(totals, inputs):
        row_tokens, row_cot, row_order, row_lengths = inputs
        offsets = (jnp.cumsum(row_lengths) - row_lengths).astype(jnp.int32)
        keep_list = keep_masks(positions, offsets)
        packed = jnp.take(row_tokens, row_order, axis=0).astype(jnp.float32)
        packed_cot = jnp.take(row_cot, row_order, axis=0).astype(jnp.float32)
        result, pullback = jax.vjp(lambda weights_in, values: stream_pass(weights_in, values, keep_list), weights_all, packed)
        grad_weights, grad_input = pullback(packed_cot)
        out_rows = jnp.zeros((CTX_TOK, D), jnp.bfloat16).at[row_order].set(result.astype(jnp.bfloat16))
        back_rows = jnp.zeros((CTX_TOK, D), jnp.bfloat16).at[row_order].set(grad_input.astype(jnp.bfloat16))
        totals = jax.tree.map(lambda acc_value, grad_value: acc_value + grad_value, totals, grad_weights)
        return (totals, (out_rows, back_rows))
    start_totals = jax.tree.map(jnp.zeros_like, weights_all)
    totals, (out_all, back_all) = lax.scan(one_stream, start_totals, (flat_tokens, flat_cot, flat_order, flat_lengths))
    return (out_all.reshape(tokens.shape), back_all.reshape(tokens.shape), totals[0], totals[1].reshape(N_TP, D // N_TP, KERNEL), totals[2], totals[3], totals[4], totals[5], totals[6], totals[7])
```

```python
import jax
import jax.numpy as jnp
from jax import lax
from jax.sharding import PartitionSpec as P

norm_eps = 1e-05
bf16 = jnp.bfloat16
f32 = jnp.float32


def pairs(count, flip):
    return [(source, source ^ flip) for source in range(count)]


def tp_sum(partial):
    own = lax.optimization_barrier(partial.astype(bf16))
    count = lax.axis_size("tp")
    total = own.astype(f32)
    step = 1
    while step < count:
        sent = own if step == 1 else total.astype(bf16)
        other = lax.ppermute(sent, "tp", pairs(count, step))
        total = sent.astype(f32) + other.astype(f32)
        step *= 2
    return total


def small_sum(value):
    for axis in ("fsdp", "ctx"):
        count = lax.axis_size(axis)
        step = 1
        while step < count:
            value = value + lax.ppermute(value, axis, pairs(count, step))
            step *= 2
    return value


def line_gather(value):
    count = lax.axis_size("ctx")
    up = [(i, i + 1) for i in range(count - 1)]
    down = [(i + 1, i) for i in range(count - 1)]
    low, high = [value], [value]
    for _ in range(count - 1):
        low.append(lax.ppermute(low[-1], "ctx", up))
        high.append(lax.ppermute(high[-1], "ctx", down))
    return [value] + [low[s] + high[count - s] for s in range(1, count)]


def neighbour_columns(order, lengths, first_row, row_count, kernel):
    total = order.shape[1]
    me, count = lax.axis_index("ctx"), lax.axis_size("ctx")
    offsets = jnp.cumsum(lengths, axis=1) - lengths
    positions = jnp.arange(total, dtype=jnp.int32)
    start = jnp.any(positions[None, :, None] == offsets[:, None, :], axis=-1)

    def back(values, steps, fill):
        return jnp.pad(values, ((0, 0), (steps, 0)), constant_values=fill)[:, :total]

    def ahead(values, steps, fill):
        return jnp.pad(values, ((0, 0), (0, steps)), constant_values=fill)[:, steps:]

    tables = []
    keep = jnp.ones(order.shape, bool)
    for lag in range(1, kernel):
        keep = keep & ~back(start, lag - 1, False)
        tables.append(jnp.where(keep, back(order, lag, -1), -1))
        tables.append(jnp.where(ahead(keep, lag, False), ahead(order, lag, -1), -1))
    rows = first_row + jnp.arange(row_count, dtype=jnp.int32)
    hit = order[:, None, :] == rows[None, :, None]
    columns = []
    for table in tables:
        wanted = jnp.sum(jnp.where(hit, table[:, None, :], 0), axis=-1)
        block = lax.rem(me - wanted // row_count + count, count)
        column = block * row_count + lax.rem(wanted, row_count)
        columns.append(jnp.where(wanted >= 0, column, -1))
    return columns[0::2], columns[1::2]


def one_hot(columns, total):
    spots = jnp.arange(total, dtype=jnp.int32)
    return jnp.concatenate([c[:, :, None] == spots for c in columns], axis=1).astype(bf16)


def pick(hot, value, micro_count, lags):
    blocks = [b.reshape(micro_count, -1, b.shape[-1]) for b in line_gather(value)]
    table = jnp.concatenate(blocks, axis=1)
    picked = jnp.einsum("mqr,mrc->mqc", hot, table, preferred_element_type=f32)
    parts = jnp.split(picked, lags, axis=1)
    return [p.reshape(value.shape) for p in parts]


def scatter_sum(grad):
    part = lax.psum_scatter(grad.astype(bf16), "fsdp", scatter_dimension=0, tiled=True)
    return lax.psum_scatter(part, "ctx", scatter_dimension=0, tiled=True).astype(f32)


def norm_back(values, scale, gain, grad_normed):
    weighted = grad_normed * gain
    return scale * weighted - values * scale**3 * jnp.mean(weighted * values, axis=1, keepdims=True)


def shards(
    tokens,
    doc_lengths,
    token_order,
    mixer_gain,
    in_weight,
    conv_kernel,
    out_weight,
    feed_gain,
    gate_weight,
    up_weight,
    down_weight,
    cotangent,
):
    micro_count, _, row_count, width = tokens.shape
    kernel = conv_kernel.shape[1]
    chans = conv_kernel.shape[0]
    total_rows = token_order.shape[2]
    first_row = lax.axis_index("ctx") * row_count
    flat = micro_count * row_count

    def gathered(weight):
        return lax.all_gather(weight, "fsdp", axis=0, tiled=True)

    in_full = gathered(in_weight)
    out_full = gathered(out_weight)
    gate_full = gathered(gate_weight)
    up_full = gathered(up_weight)
    down_full = gathered(down_weight)
    gains = lax.all_gather(jnp.stack([mixer_gain, feed_gain]), "fsdp", axis=1, tiled=True)
    gain_one = gains[0].astype(f32)
    gain_two = gains[1].astype(f32)
    taps = conv_kernel.astype(f32)

    back_cols, ahead_cols = neighbour_columns(
        token_order[:, 0], doc_lengths[:, 0], first_row, row_count, kernel
    )
    back_hot = one_hot(back_cols, total_rows)
    ahead_hot = one_hot(ahead_cols, total_rows)

    def mm(a, b):
        return jnp.dot(a, b, preferred_element_type=f32)

    def mm_t(a, b):
        return jnp.einsum("pc,oc->po", a, b, preferred_element_type=f32)

    def outer(a, b):
        return jnp.einsum("po,pf->of", a, b, preferred_element_type=f32)

    rows = tokens.reshape(flat, width).astype(f32)
    d_out = cotangent.reshape(flat, width)
    scale_one = lax.rsqrt(jnp.mean(rows * rows, axis=1, keepdims=True) + norm_eps)
    normed_one = (rows * scale_one * gain_one).astype(bf16)
    b_part = mm(normed_one, in_full[:, 0])
    x_part = mm(normed_one, in_full[:, 2])
    mixed_in = b_part * x_part
    c_part = mm(normed_one, in_full[:, 1])
    lagged = pick(back_hot, mixed_in.astype(bf16), micro_count, kernel - 1)
    conv_out = mixed_in * taps[:, 0]
    for lag in range(1, kernel):
        conv_out = conv_out + lagged[lag - 1] * taps[:, lag]
    gated = (c_part * conv_out).astype(bf16)
    resid = rows + tp_sum(mm_t(gated, out_full))
    scale_two = lax.rsqrt(jnp.mean(resid * resid, axis=1, keepdims=True) + norm_eps)
    normed_two = (resid * scale_two * gain_two).astype(bf16)
    gate_proj = mm(normed_two, gate_full)
    up_proj = mm(normed_two, up_full)
    sigmoid_g = jax.nn.sigmoid(gate_proj)
    silu_gate = gate_proj * sigmoid_g
    hidden = (silu_gate * up_proj).astype(bf16)
    down_grad = scatter_sum(outer(d_out, hidden))
    block_rows = (resid + tp_sum(mm_t(hidden, down_full))).astype(bf16)
    d_hidden = mm(d_out, down_full)
    d_gate = (d_hidden * up_proj * sigmoid_g * (1.0 + gate_proj * (1.0 - sigmoid_g))).astype(bf16)
    d_up = (d_hidden * silu_gate).astype(bf16)
    d_normed_two = tp_sum(mm_t(d_gate, gate_full) + mm_t(d_up, up_full))
    gate_grad = scatter_sum(outer(normed_two, d_gate))
    up_grad = scatter_sum(outer(normed_two, d_up))
    feed_part = jnp.sum(d_normed_two * resid * scale_two, axis=0)
    d_resid = d_out.astype(f32) + norm_back(resid, scale_two, gain_two, d_normed_two)
    d_branch = d_resid.astype(bf16)
    out_grad = scatter_sum(outer(d_branch, gated))
    d_gated = mm(d_branch, out_full)
    d_cpart = d_gated * conv_out
    d_conv = d_gated * c_part
    later = pick(ahead_hot, d_conv.astype(bf16), micro_count, kernel - 1)
    d_mixed = d_conv * taps[:, 0]
    kernel_terms = [jnp.sum(d_conv * mixed_in, axis=0)]
    for lag in range(1, kernel):
        d_mixed = d_mixed + later[lag - 1] * taps[:, lag]
        kernel_terms.append(jnp.sum(d_conv * lagged[lag - 1], axis=0))
    d_b = (d_mixed * x_part).astype(bf16)
    d_c = d_cpart.astype(bf16)
    d_x = (d_mixed * b_part).astype(bf16)
    in_grad = scatter_sum(
        jnp.concatenate([outer(normed_one, d_b), outer(normed_one, d_c), outer(normed_one, d_x)], 1)
    )
    part_one = mm_t(d_b, in_full[:, 0]) + mm_t(d_c, in_full[:, 1]) + mm_t(d_x, in_full[:, 2])
    d_normed_one = tp_sum(part_one)
    mixer_part = jnp.sum(d_normed_one * rows * scale_one, axis=0)
    grad_rows = (d_resid + norm_back(rows, scale_one, gain_one, d_normed_one)).astype(bf16)

    small = small_sum(jnp.concatenate([mixer_part, feed_part] + kernel_terms))
    shard = lax.axis_index("fsdp") * lax.axis_size("ctx") + lax.axis_index("ctx")
    shard_count = lax.axis_size("fsdp") * lax.axis_size("ctx")

    def piece(value, axis=0):
        size = value.shape[axis] // shard_count
        return lax.dynamic_slice_in_dim(value, shard * size, size, axis)

    mixer_grad = piece(small[:width])
    feed_grad = piece(small[width : 2 * width])
    kernel_grad = piece(small[2 * width :].reshape(kernel, chans), 1).T[None]
    shape = tokens.shape
    return (
        block_rows.reshape(shape),
        grad_rows.reshape(shape),
        in_grad.reshape(in_grad.shape[0], 3, chans),
        kernel_grad,
        out_grad,
        gate_grad,
        up_grad,
        down_grad,
        mixer_grad,
        feed_grad,
    )


def solution(mesh):
    return jax.shard_map(
        shards,
        mesh=mesh,
        in_specs=(
            P(None, "fsdp", "ctx", None),
            P(None, "fsdp", None),
            P(None, "fsdp", None),
            P("fsdp"),
            P("fsdp", None, "tp"),
            P("tp", None),
            P("fsdp", "tp"),
            P("fsdp"),
            P("fsdp", "tp"),
            P("fsdp", "tp"),
            P("fsdp", "tp"),
            P(None, "fsdp", "ctx", None),
        ),
        out_specs=(
            P(None, "fsdp", "ctx", None),
            P(None, "fsdp", "ctx", None),
            P(("fsdp", "ctx"), None, "tp"),
            P("tp", ("fsdp", "ctx"), None),
            P(("fsdp", "ctx"), "tp"),
            P(("fsdp", "ctx"), "tp"),
            P(("fsdp", "ctx"), "tp"),
            P(("fsdp", "ctx"), "tp"),
            P(("fsdp", "ctx")),
            P(("fsdp", "ctx")),
        ),
        check_vma=False,
    )
```
